32 devices in a mesh: seq: 16 (over z, y, x), mp: 2 (over core).
Axes of the slice: x: 2, y: 2, z: 4, core: 2. Of those that a mesh axis runs over, the one named last changes fastest.
Arguments:
- stream: bfloat16 [8192, 2048], P('seq'), may hold values from -6 to 6
- doc_ids: int32 [8192], P('seq'), may hold values from 0 to 7, never falling along the last dimension, each value on 1 to 4096 neighbouring positions
- valid_mask: int32 [8192], P('seq'), may hold values 0 or 1
- mixer_gain: float32 [2048], replicated, may hold values from 0.5 to 1.5
- branch_proj: bfloat16 [2048, 2560], P(None, 'mp'), may hold values from -0.125 to 0.125
- input_proj: bfloat16 [2048, 2560], P(None, 'mp'), may hold values from -0.125 to 0.125
- conv_kernel: float32 [4, 10, 256], P(None, 'mp'), may hold values from -3 to 3
- conv_bias: float32 [10, 256], P('mp'), may hold values from -2 to 2
- decay_gates: bfloat16 [10, 256, 256], P('mp'), may hold values from -0.375 to 0.375
- decay_bias: float32 [10, 256], P('mp'), may hold values from -4 to 4
- input_gates: bfloat16 [10, 256, 256], P('mp'), may hold values from -0.375 to 0.375
- input_bias: float32 [10, 256], P('mp'), may hold values from -4 to 4
- decay_rate: float32 [10, 256], P('mp'), may hold values from 1e-05 to 0.1
- output_proj: bfloat16 [2560, 2048], P('mp'), may hold values from -0.3125 to 0.3125
- ffn_gain: float32 [2048], replicated, may hold values from 0.5 to 1.5
- gate_proj: bfloat16 [2048, 6144], P(None, 'mp'), may hold values from -0.125 to 0.125
- up_proj: bfloat16 [2048, 6144], P(None, 'mp'), may hold values from -0.125 to 0.125
- down_proj: bfloat16 [6144, 2048], P('mp'), may hold values from -0.15625 to 0.15625
- out_grad: bfloat16 [8192, 2048], P('seq'), may hold values from -6 to 6
Outputs:
- result: float32 [8192, 2048], P('seq')
- stream_grad: float32 [8192, 2048], P('seq')
- mixer_gain_grad: float32 [2048], P('seq')
- branch_proj_grad: float32 [2048, 2560], P('seq', 'mp')
- input_proj_grad: float32 [2048, 2560], P('seq', 'mp')
- conv_kernel_grad: float32 [4, 10, 256], P(None, 'mp', 'seq')
- conv_bias_grad: float32 [10, 256], P('mp', 'seq')
- decay_gates_grad: float32 [10, 256, 256], P('mp', 'seq')
- decay_bias_grad: float32 [10, 256], P('mp', 'seq')
- input_gates_grad: float32 [10, 256, 256], P('mp', 'seq')
- input_bias_grad: float32 [10, 256], P('mp', 'seq')
- decay_rate_grad: float32 [10, 256], P('mp', 'seq')
- output_proj_grad: float32 [2560, 2048], P('mp', 'seq')
- ffn_gain_grad: float32 [2048], P('seq')
- gate_proj_grad: float32 [2048, 6144], P('seq', 'mp')
- up_proj_grad: float32 [2048, 6144], P('seq', 'mp')
- down_proj_grad: float32 [6144, 2048], P('mp', 'seq')
The draws below stay inside these ranges and needn't reach their ends.
Inputs may be any that keep to these rules, and one draw needn't show every extreme that they name: `doc_ids`: document ids of the packed stream start at 0 and never fall; every document has 1 to 4096 tokens and one has exactly 4096.
All inputs are finite; a program needn't handle non-finite values. No bound on the sum of `valid_mask` on one device may be relied on, other than what follows from the above.
Results may differ from the reference program's by a relative error of at most 0.013.
Values sent between devices are 32-bit elements; how exact they have to be, the bound alone decides.
No kernel may reach another device: no remote copies, remote signals or barrier semaphores. Data moves between devices by JAX's collectives and lax.ppermute only.
A program may use at most 320 MiB of HBM per device.

```python
import math
import jax
import jax.numpy as jnp
import numpy as np
from jax import lax

D = 2048
BLOCKS = 10
BLOCK = 256
FF = 6144
CONV = 4
W = 2560
TOKENS = 8192
DOCS = 8
MOST_DOC = 4096


def set_ends(array, rng, low, high):
    shape = array.shape
    place = [jax.random.randint(jax.random.fold_in(rng, axis), (), 0, shape[axis]) for axis in range(len(shape))]
    array = array.at[tuple(place)].set(low)
    longest = shape.index(max(shape))
    place[longest] = (place[longest] + 1) % shape[longest]
    return array.at[tuple(place)].set(high)


def level_of(stream_key, extent, shards, least, largest):
    level, own = 1.0, jax.random.fold_in(stream_key, 6)
    for axis_at, parts in shards:
        steps = jnp.exp(jax.random.uniform(jax.random.fold_in(own, axis_at), (parts,), jnp.float32, least / len(shards), largest / len(shards)))
        level = level * jnp.repeat(steps, extent[axis_at] // parts).reshape([-1 if axis == axis_at else 1 for axis in range(len(extent))])
    return level


def profile(amount, total, limit, lean):
    weights = [(1 << 20) // math.isqrt(standing ** lean) + 1 for standing in range(2, amount + 1)]
    surplus, holding = total - limit - (amount - 1), [1] * (amount - 1)
    while surplus > 0:
        movable = [i for i in range(amount - 1) if holding[i] < limit]
        mass, budget = sum([weights[i] for i in movable]), surplus
        for i in movable:
            more = min(limit - holding[i], max(1, budget * weights[i] // mass), surplus)
            holding[i] = holding[i] + more
            surplus = surplus - more
    return np.array([limit] + holding)


def uneven(stream_key, amount, total, limit, lean):
    if amount == 2:
        one = jax.random.randint(stream_key, (), max(1, total - limit), min(limit, total - 1) + 1)
        return jnp.stack([one, total - one])
    tallies = jnp.asarray(profile(amount, total, limit, lean), jnp.int32)
    couples = (amount - 1) // 2
    donor, receiver = tallies[1:1 + 2 * couples:2], tallies[2:2 + 2 * couples:2]
    room = jnp.minimum(donor - 1, limit - receiver)
    passed = jax.random.randint(jax.random.fold_in(stream_key, 1), (couples,), 0, 1 << 20) % (room + 1)
    tallies = tallies.at[1:1 + 2 * couples:2].set(donor - passed).at[2:2 + 2 * couples:2].set(receiver + passed)
    return tallies[jax.random.permutation(jax.random.fold_in(stream_key, 2), amount)]


def normal_values(own_key, dims, scale, reach, shards=(), dtype=jnp.bfloat16):
    loudness = level_of(own_key, dims, shards, -0.22, 0.18) if shards else 1.0
    drawn = jax.random.normal(own_key, dims, jnp.float32) * scale * loudness
    return jnp.minimum(jnp.maximum(drawn, -reach), reach).astype(dtype)


def setup_inputs(seed: int = 0) -> dict:
    splits = jax.random.split(jax.random.key(seed), 20)
    stream = normal_values(splits[0], (TOKENS, D), 1.0, 6.0, ((0, 16),))
    doc_ids = jnp.searchsorted(jnp.cumsum(uneven(splits[1], DOCS, TOKENS, MOST_DOC, 2)), jnp.arange(TOKENS), side="right").astype(jnp.int32)
    valid_mask = set_ends((jax.random.randint(splits[2], (TOKENS,), 0, 8) < 7).astype(jnp.int32), jax.random.fold_in(splits[2], 1), 0, 1)
    mixer_gain = jnp.clip(1.0 + 0.1 * jax.random.normal(splits[3], (D,), jnp.float32), 0.5, 1.5)
    branch_proj = normal_values(splits[4], (D, W), D ** -0.5, 0.125, ((1, 2),))
    input_proj = normal_values(splits[5], (D, W), D ** -0.5, 0.125, ((1, 2),))
    conv_kernel = normal_values(splits[6], (CONV, BLOCKS, BLOCK), 0.5, 3.0, ((1, 2),), jnp.float32)
    conv_bias = normal_values(splits[7], (BLOCKS, BLOCK), 0.3, 2.0, ((0, 2),), jnp.float32)
    decay_gates = normal_values(splits[8], (BLOCKS, BLOCK, BLOCK), BLOCK ** -0.5, 0.375, ((0, 2),))
    decay_bias = normal_values(splits[9], (BLOCKS, BLOCK), 1.0, 4.0, ((0, 2),), jnp.float32)
    input_gates = normal_values(splits[10], (BLOCKS, BLOCK, BLOCK), BLOCK ** -0.5, 0.375, ((0, 2),))
    input_bias = normal_values(splits[11], (BLOCKS, BLOCK), 1.0, 4.0, ((0, 2),), jnp.float32)
    decay_rate = jnp.clip(jnp.exp(math.log(0.1) - 9.2103404 * jax.random.uniform(splits[12], (BLOCKS, BLOCK), jnp.float32) ** level_of(splits[12], (BLOCKS, BLOCK), ((0, 2),), -0.2, 0.2)), 9.999999747378752e-06, 0.1)
    output_proj = normal_values(splits[13], (W, D), (W // 8) ** -0.5, 0.3125, ((0, 2),))
    ffn_gain = jnp.clip(1.0 + 0.1 * jax.random.normal(splits[14], (D,), jnp.float32), 0.5, 1.5)
    gate_proj = normal_values(splits[15], (D, FF), D ** -0.5, 0.125, ((1, 2),))
    up_proj = normal_values(splits[16], (D, FF), D ** -0.5, 0.125, ((1, 2),))
    down_proj = normal_values(splits[17], (FF, D), (FF // 4) ** -0.5, 0.15625, ((0, 2),))
    out_grad = normal_values(splits[18], (TOKENS, D), 1.0, 6.0, ((0, 16),))
    return {"stream": stream, "doc_ids": doc_ids, "valid_mask": valid_mask, "mixer_gain": mixer_gain, "branch_proj": branch_proj, "input_proj": input_proj, "conv_kernel": conv_kernel, "conv_bias": conv_bias, "decay_gates": decay_gates, "decay_bias": decay_bias, "input_gates": input_gates, "input_bias": input_bias, "decay_rate": decay_rate, "output_proj": output_proj, "ffn_gain": ffn_gain, "gate_proj": gate_proj, "up_proj": up_proj, "down_proj": down_proj, "out_grad": out_grad}


EPS = 1e-06
HIGH = lax.Precision.HIGHEST

@jax.custom_vjp
def low(v):
    return lax.optimization_barrier(v.astype(jnp.bfloat16)).astype(jnp.float32)

@jax.custom_vjp
def low_back(v):
    return v

def low_keep(v):
    return (low(v), None)

def low_pass(kept, grad):
    return (grad,)

def back_keep(v):
    return (v, None)

def back_low(kept, grad):
    return (low(grad),)
low.defvjp(low_keep, low_pass)
low_back.defvjp(back_keep, back_low)

def matmul(left, right):
    return jnp.dot(left, right, precision=HIGH)

def rms_norm(values, gain):
    factor = lax.rsqrt(lax.optimization_barrier(jnp.mean(values * values, axis=-1, keepdims=True)) + EPS)
    return values * factor * gain

def recurrence(decays, inputs):
    span = math.gcd(decays.shape[0], 512)
    width = decays.shape[1]
    dec_blocks = decays.reshape(-1, span, width)
    inp_blocks = inputs.reshape(-1, span, width)

    def inner(state, pair):
        state = pair[0] * state + pair[1]
        return (state, state)

    @jax.checkpoint
    def outer(state, pair):
        return lax.scan(inner, state, pair)
    final, states = lax.scan(outer, jnp.zeros((width,), jnp.float32), (dec_blocks, inp_blocks))
    return states.reshape(-1, width)

def forward(params, reset, same, valid):
    stream, mixer_gain, branch_proj, input_proj, conv_kernel, conv_bias, decay_gates, decay_bias, input_gates, input_bias, decay_rate, output_proj, ffn_gain, gate_proj, up_proj, down_proj = params
    normed = low(rms_norm(stream, mixer_gain))
    branch_act = jax.nn.gelu(low_back(matmul(normed, branch_proj)))
    signal = low(low_back(matmul(normed, input_proj)))
    padded = jnp.concatenate([jnp.zeros((CONV - 1, W), jnp.float32), signal], 0)
    kernel = conv_kernel.reshape(CONV, W)
    conv = conv_bias.reshape(W)
    for shift in range(CONV):
        conv = conv + kernel[shift] * padded[CONV - 1 - shift:CONV - 1 - shift + TOKENS] * same[shift]
    conv_low = low(conv).reshape(TOKENS, BLOCKS, BLOCK)
    decay_pre = low_back(jnp.einsum('tbi,bij->tbj', conv_low, decay_gates, precision=HIGH) + decay_bias)
    input_pre = low_back(jnp.einsum('tbi,bij->tbj', conv_low, input_gates, precision=HIGH) + input_bias)
    rgate = jax.nn.sigmoid(decay_pre).reshape(TOKENS, W)
    igate = jax.nn.sigmoid(input_pre).reshape(TOKENS, W)
    log_decay = -8.0 * rgate * decay_rate.reshape(W)
    decay = jnp.exp(log_decay)
    scale = jnp.sqrt(-jnp.expm1(2.0 * log_decay))
    multiplier = (1.0 - reset) * (valid * decay + 1.0 - valid)
    inputs = valid * scale * igate * conv
    states = recurrence(multiplier, inputs)
    mixed = low(states * branch_act)
    middle = stream + low_back(matmul(mixed, output_proj))
    normed_ffn = low(rms_norm(middle, ffn_gain))
    gate = low_back(matmul(normed_ffn, gate_proj))
    upward = low_back(matmul(normed_ffn, up_proj))
    hidden = low(jax.nn.gelu(gate) * upward)
    return middle + low_back(matmul(hidden, down_proj))

def reference(stream, doc_ids, valid_mask, mixer_gain, branch_proj, input_proj, conv_kernel, conv_bias, decay_gates, decay_bias, input_gates, input_bias, decay_rate, output_proj, ffn_gain, gate_proj, up_proj, down_proj, out_grad):
    previous = jnp.concatenate([doc_ids[:1] - 1, doc_ids[:-1]], 0)
    reset = (doc_ids != previous).astype(jnp.float32)[:, None]
    same = []
    for shift in range(CONV):
        earlier = jnp.concatenate([jnp.full((shift,), -1, jnp.int32), doc_ids[:TOKENS - shift].astype(jnp.int32)], 0)
        same.append((earlier == doc_ids).astype(jnp.float32)[:, None])
    valid = valid_mask.astype(jnp.float32)[:, None]
    floats = tuple((item.astype(jnp.float32) for item in (stream, mixer_gain, branch_proj, input_proj, conv_kernel, conv_bias, decay_gates, decay_bias, input_gates, input_bias, decay_rate, output_proj, ffn_gain, gate_proj, up_proj, down_proj)))
    result, pullback = jax.vjp(lambda *params: forward(params, reset, same, valid), *floats)
    grads = pullback(out_grad.astype(jnp.float32))
    return (result, grads[0], grads[1], grads[2], grads[3], grads[4], grads[5], grads[6], grads[7], grads[8], grads[9], grads[10], grads[11], grads[12], grads[13], grads[14], grads[15])
```

```python
import functools

import jax
import jax.numpy as jnp
from jax import lax
from jax.experimental import pallas as pl
from jax.experimental.pallas import tpu as pltpu
from jax.sharding import PartitionSpec as P

EPS = 1e-06
GATE_SCALE = 8.0
MOST_DOC = 4096
GELU_C = 0.7978845608028654
GELU_A = 0.044715
HALO = 8
SEG = 8


F32 = jnp.float32
BF16 = jnp.bfloat16


def shift_route(peers, distance):
    return [(i - distance, i) for i in range(peers) if 0 <= i - distance < peers]


def seq_shift(value, distance):
    return lax.ppermute(value, "seq", shift_route(lax.axis_size("seq"), distance))


def seq_flip(value, bit):
    peers = lax.axis_size("seq")
    return lax.ppermute(value, "seq", [(i, i ^ (1 << bit)) for i in range(peers)])


def mp_swap(value):
    return lax.ppermute(value, "mp", [(0, 1), (1, 0)])


def mp_sum(value):
    return value + mp_swap(value)


def carried_in(product, state, sign, rows):
    peers = lax.axis_size("seq")
    reach = min(peers - 1, -(-MOST_DOC // rows))
    pair = seq_shift(jnp.stack([product, state]), sign)
    span = 1
    while span < reach:
        far = seq_shift(pair, sign * span)
        pair = jnp.stack([pair[0] * far[0], pair[0] * far[1] + pair[1]])
        span *= 2
    return pair[1]


def rms_scale(values):
    return lax.rsqrt(jnp.mean(values * values, axis=-1, keepdims=True) + EPS)


def norm_back(weighted, values, factor):
    return factor * weighted - values * factor**3 * jnp.mean(
        weighted * values, axis=-1, keepdims=True
    )


def gelu_parts(v):
    square = v * v
    t = jnp.tanh(GELU_C * v * (1.0 + GELU_A * square))
    value = 0.5 * v * (1.0 + t)
    slope = 0.5 * (1.0 + t) + 0.5 * v * (1.0 - t * t) * GELU_C * (1.0 + 3.0 * GELU_A * square)
    return value, slope


def one_minus_exp(v):
    series = 1.0 + v * (1.0 / 8.0)
    for k in (7.0, 6.0, 5.0, 4.0, 3.0, 2.0):
        series = 1.0 + v * (1.0 / k) * series
    return jnp.where(v > -0.5, -v * series, 1.0 - jnp.exp(v))


def sigmoid(v):
    return 1.0 / (1.0 + jnp.exp(-v))


def cell(rgate, rate):
    log_decay = -GATE_SCALE * rgate * rate
    return jnp.exp(log_decay), jnp.sqrt(one_minus_exp(2.0 * log_decay))


def scan_pass(mult, inp, local, prod, local_o, prod_o, offset, reverse):
    lanes, rows = inp.shape[0], inp.shape[1]
    steps = rows // SEG

    def turn(k, pairs):
        j = steps - 1 - k if reverse else k
        at = pl.ds(j, SEG, stride=steps)
        out = []
        for h in range(lanes):
            a = mult[h, pl.ds(j + offset, SEG, stride=steps), :]
            state = a * pairs[h][0] + inp[h, at, :]
            run = a * pairs[h][1]
            local[h, at, :] = state
            prod[h, at, :] = run
            out.append((state, run))
        return tuple(out)

    zero = jnp.zeros((SEG, 128), F32)
    ends = lax.fori_loop(0, steps, turn, ((zero, zero + 1.0),) * lanes, unroll=8)
    for h in range(lanes):
        state, run = ends[h]
        carry = jnp.zeros((1, 128), F32)
        ahead = carry + 1.0
        for s in reversed(range(SEG)) if reverse else range(SEG):
            at = pl.ds(s * steps, steps)
            to = pl.ds(h * 128, 128)
            part = prod[h, at, :]
            local_o[at, to] = local[h, at, :] + part * carry
            prod_o[at, to] = part * ahead
            carry = run[s : s + 1] * carry + state[s : s + 1]
            ahead = run[s : s + 1] * ahead


def put_lanes(ref, rows, value):
    for h in range(ref.shape[0]):
        ref[h, rows, :] = value[:, h * 128 : (h + 1) * 128]


def forward_kernel(
    signal, edge, masks, params, dgate, igate_w, conv_o, rgate_o, igate_o, mult_o, local_o, prod_o, ext, step, inp, local, prod
):
    rows, cols = signal.shape
    ext[0:HALO, :] = edge[...]
    ext[HALO:, :] = signal[...].astype(F32)
    conv = params[4:5, :] + params[0:1, :] * ext[HALO:, :]
    for k in (1, 2, 3):
        conv = conv + params[k : k + 1, :] * ext[pl.ds(HALO - k, rows), :] * masks[:, k - 1 : k]
    conv_o[...] = conv
    low = conv.astype(BF16)
    rgate = sigmoid(jnp.dot(low, dgate[...], preferred_element_type=F32) + params[5:6, :])
    igate = sigmoid(jnp.dot(low, igate_w[...], preferred_element_type=F32) + params[6:7, :])
    rgate_o[...] = rgate
    igate_o[...] = igate
    decay, scale = cell(rgate, params[7:8, :])
    valid, keep = masks[:, 3:4], masks[:, 4:5]
    mult = keep * (valid * decay + (1.0 - valid))
    mult_o[...] = mult
    put_lanes(step, pl.ds(0, rows), mult)
    put_lanes(inp, pl.ds(0, rows), valid * scale * igate * conv)
    scan_pass(step, inp, local, prod, local_o, prod_o, 0, False)


def reverse_kernel(mixed_grad, branch_pre, states, mult, branch_grad_o, local_o, prod_o, step, inp, local, prod):
    rows, cols = mixed_grad.shape
    act, slope = gelu_parts(branch_pre[...])
    grad = mixed_grad[...]
    branch_grad_o[...] = (slope * (grad * states[...])).astype(BF16)
    put_lanes(inp, pl.ds(0, rows), grad * act)
    put_lanes(step, pl.ds(0, rows), mult[...])
    put_lanes(step, pl.ds(rows, HALO), jnp.ones((HALO, cols), F32))
    scan_pass(step, inp, local, prod, local_o, prod_o, 1, True)


def backward_kernel(
    local,
    suffix,
    adj_in,
    states,
    carry_in,
    conv_r,
    rgate_r,
    igate_r,
    signal,
    edge,
    masks,
    params,
    dgate,
    igate_w,
    signal_grad_o,
    edge_o,
    dgate_o,
    igate_o,
    sums_o,
    prev,
    ext,
    buf,
):
    rows, cols = local.shape
    adjoint = local[...] + suffix[...] * adj_in[0:1, :]
    prev[0:HALO, :] = jnp.broadcast_to(carry_in[0:1, :], (HALO, cols))
    prev[HALO:, :] = states[...]
    state_prev = prev[pl.ds(HALO - 1, rows), :]
    conv, rgate, igate = conv_r[...], rgate_r[...], igate_r[...]
    rate = params[7:8, :]
    decay, scale = cell(rgate, rate)
    valid, keep = masks[:, 3:4], masks[:, 4:5]
    av = adjoint * valid
    gated = av * conv * igate
    log_grad = av * state_prev * keep * decay - gated * decay * decay / scale
    scaled = -GATE_SCALE * rgate * log_grad
    dpg = (scaled * rate * (1.0 - rgate)).astype(BF16)
    ipg = (gated * scale * (1.0 - igate)).astype(BF16)
    low = conv.astype(BF16)
    over_tokens = (((0,), (0,)), ((), ()))
    dgate_o[...] = lax.dot_general(low, dpg, over_tokens, preferred_element_type=F32)
    igate_o[...] = lax.dot_general(low, ipg, over_tokens, preferred_element_type=F32)
    back = (((1,), (1,)), ((), ()))
    conv_grad = (
        av * scale * igate
        + lax.dot_general(dpg, dgate[...], back, preferred_element_type=F32)
        + lax.dot_general(ipg, igate_w[...], back, preferred_element_type=F32)
    )
    ext[0:HALO, :] = edge[...]
    ext[HALO:, :] = signal[...].astype(F32)

    def total(v):
        return jnp.sum(v, axis=0, keepdims=True)

    sums_o[0:1, :] = total(conv_grad * ext[HALO:, :])
    buf[0:HALO, :] = jnp.zeros((HALO, cols), F32)
    buf[rows + HALO :, :] = jnp.zeros((HALO, cols), F32)
    buf[pl.ds(HALO, rows), :] = conv_grad * params[0:1, :]
    acc = buf[0 : rows + HALO, :]
    for k in (1, 2, 3):
        seen = conv_grad * masks[:, k - 1 : k]
        sums_o[k : k + 1, :] = total(seen * ext[pl.ds(HALO - k, rows), :])
        buf[pl.ds(HALO, rows), :] = seen * params[k : k + 1, :]
        acc = acc + buf[pl.ds(k, rows + HALO), :]
    edge_o[...] = acc[0:HALO]
    signal_grad_o[...] = acc[HALO:]
    sums_o[4:5, :] = total(conv_grad)
    sums_o[5:6, :] = total(dpg.astype(F32))
    sums_o[6:7, :] = total(ipg.astype(F32))
    sums_o[7:8, :] = total(scaled)


def per_block(kernel, rows, blocks, block, ins, outs, scratch, lanes, flops, args):
    def spec(kind):
        if kind == "gate":
            return pl.BlockSpec((None, block, block), lambda b: (b, 0, 0))
        if kind == "mask":
            return pl.BlockSpec((rows, 128), lambda b: (0, 0))
        if kind == "edge":
            return pl.BlockSpec((HALO, block), lambda b: (0, b))
        return pl.BlockSpec((rows, block), lambda b: (0, b))

    def shape(kind):
        width = blocks * block
        if kind == "gate":
            return jax.ShapeDtypeStruct((blocks, block, block), F32)
        if kind == "edge":
            return jax.ShapeDtypeStruct((HALO, width), F32)
        return jax.ShapeDtypeStruct((rows, width), BF16 if kind == "low" else F32)

    size = rows * blocks * block
    return pl.pallas_call(
        kernel,
        grid=(blocks,),
        in_specs=[spec(k) for k in ins],
        out_specs=[spec(k) for k in outs],
        out_shape=[shape(k) for k in outs],
        scratch_shapes=[pltpu.VMEM((rows + extra, block), F32) for extra in scratch]
        + [pltpu.VMEM((block // 128, rows + extra, 128), F32) for extra in lanes],
        compiler_params=pltpu.CompilerParams(vmem_limit_bytes=56 * 2**20),
        cost_estimate=pl.CostEstimate(
            flops=flops * size,
            transcendentals=4 * size,
            bytes_accessed=4 * size * (len(ins) + len(outs)),
        ),
    )(*args)


def take_columns_kernel(at, source, out):
    out[...] = source[...]


def take_columns(values, blocks_at, count, wide):
    rows = values.shape[0]
    if wide % 128:
        return values.reshape(rows, count, wide)[:, blocks_at].reshape(rows, count * wide)
    return pl.pallas_call(
        take_columns_kernel,
        grid_spec=pltpu.PrefetchScalarGridSpec(
            num_scalar_prefetch=1,
            grid=(count,),
            in_specs=[pl.BlockSpec((rows, wide), lambda p, at: (0, at[p]))],
            out_specs=pl.BlockSpec((rows, wide), lambda p, at: (0, p)),
        ),
        out_shape=jax.ShapeDtypeStruct((rows, count * wide), values.dtype),
        cost_estimate=pl.CostEstimate(
            flops=0, transcendentals=0, bytes_accessed=4 * rows * count * wide
        ),
    )(blocks_at, values)


def ordered_blocks(order):
    count = 1 << len(order)
    return [
        sum(((p >> (len(order) - 1 - at)) & 1) << bit for at, bit in enumerate(order))
        for p in range(count)
    ]


def dot_tn(left, right):
    return lax.dot_general(left, right, (((0,), (0,)), ((), ())), preferred_element_type=F32)


def scatter_sum(partial_of, order, axis, wide):
    count = 1 << len(order)
    parts = []
    top = count
    while top > 4:
        parts.append((top // 2, top, partial_of(top // 2, top)))
        top //= 2
    parts.append((0, top, partial_of(0, top)))

    def cut(array, start, p, q):
        return lax.slice_in_dim(array, (p - start) * wide, (q - start) * wide, axis=axis)

    received = []

    def total(p, q):
        value = None
        for start, stop, array in parts:
            if start <= p and q <= stop:
                value = cut(array, start, p, q)
        for array in received:
            value = value + cut(array, 0, p, q)
        return value

    for level, bit in enumerate(order):
        received.append(seq_flip(total(count >> (level + 1), count >> level), bit))
    return total(0, 1)


def on_device(
    stream,
    doc_ids,
    valid_mask,
    mixer_gain,
    branch_proj,
    input_proj,
    conv_kernel,
    conv_bias,
    decay_gates,
    decay_bias,
    input_gates,
    input_bias,
    decay_rate,
    output_proj,
    ffn_gain,
    gate_proj,
    up_proj,
    down_proj,
    out_grad,
):
    rows = stream.shape[0]
    model = stream.shape[1]
    width = input_proj.shape[1]
    hidden_units = gate_proj.shape[1]
    blocks = decay_gates.shape[0]
    block = decay_gates.shape[1]
    taps = conv_kernel.shape[0]
    peers = lax.axis_size("seq")
    me = lax.axis_index("seq")
    bits = list(range(peers.bit_length() - 1))
    orders = {
        "x": bits[:2] + bits[2:],
        "y": bits[:2][::-1] + bits[2:],
        "z": bits[2:] + bits[:2],
    }
    wide = model // peers

    ids_float = doc_ids.astype(F32)
    id_edge = seq_shift(ids_float[rows - 128 :].reshape(1, 128), 1)[0]
    first = me == 0
    ext_ids = jnp.concatenate([jnp.where(first, -1.0, id_edge[128 - taps + 1 :]), ids_float])
    same = [
        (ext_ids[taps - 1 - k : taps - 1 - k + rows] == ids_float).astype(F32) for k in range(1, 4)
    ]
    valid = valid_mask.astype(F32)
    masks = jnp.stack(same + [valid, same[0]], axis=1)
    masks = jnp.pad(masks, ((0, 0), (0, 128 - masks.shape[1])))
    params = jnp.concatenate(
        [
            conv_kernel.reshape(taps, width),
            conv_bias.reshape(1, width),
            decay_bias.reshape(1, width),
            input_bias.reshape(1, width),
            decay_rate.reshape(1, width),
        ]
    )

    residual = stream.astype(F32)
    mix_scale = rms_scale(residual)
    mix_unit = residual * mix_scale
    normed = (mix_unit * mixer_gain).astype(BF16)
    signal = jnp.dot(normed, input_proj, preferred_element_type=F32).astype(BF16)
    edge = seq_shift(signal[rows - HALO :].astype(F32), 1)
    branch_pre = jnp.dot(normed, branch_proj, preferred_element_type=F32)
    conv, rgate, igate, mult, local_state, prefix = per_block(
        forward_kernel,
        rows,
        blocks,
        block,
        ["full", "edge", "mask", "edge", "gate", "gate"],
        ["full"] * 6,
        [HALO],
        [HALO, 0, 0, 0],
        2 * 2 * block + 60,
        (signal, edge, masks, params, decay_gates, input_gates),
    )
    carry_in = carried_in(prefix[-1:], local_state[-1:], 1, rows)
    hidden_grad = jnp.dot(out_grad, down_proj.T, preferred_element_type=F32)
    states = local_state + prefix * carry_in
    mixed = (states * jax.nn.gelu(branch_pre)).astype(BF16)
    mix_out = mp_sum(jnp.dot(mixed, output_proj, preferred_element_type=F32))
    middle = residual + mix_out

    ffn_scale = rms_scale(middle)
    ffn_unit = middle * ffn_scale
    normed_ffn = (ffn_unit * ffn_gain).astype(BF16)
    gate = jnp.dot(normed_ffn, gate_proj, preferred_element_type=F32)
    upward = jnp.dot(normed_ffn, up_proj, preferred_element_type=F32)
    gate_act, gate_slope = gelu_parts(gate)
    hidden = (gate_act * upward).astype(BF16)
    gate_grad = (hidden_grad * upward * gate_slope).astype(BF16)
    up_grad = (hidden_grad * gate_act).astype(BF16)
    result = middle + mp_sum(jnp.dot(hidden, down_proj, preferred_element_type=F32))
    ffn_part = jnp.dot(gate_grad, gate_proj.T, preferred_element_type=F32) + jnp.dot(
        up_grad, up_proj.T, preferred_element_type=F32
    )
    ffn_norm_grad = mp_sum(ffn_part)
    ffn_gain_grad = jnp.sum(ffn_norm_grad * ffn_unit, axis=0)
    middle_grad = out_grad.astype(F32) + norm_back(ffn_norm_grad * ffn_gain, middle, ffn_scale)
    mix_low = middle_grad.astype(BF16)

    def blocks_of(values, name):
        return take_columns(values, me ^ jnp.array(ordered_blocks(orders[name]), jnp.int32), peers, wide)

    def row_sum(left, right, name):
        return scatter_sum(
            lambda p, q: dot_tn(left[name][:, p * wide : q * wide], right), orders[name], 0, wide
        )

    def column_sum(left, right, name):
        return scatter_sum(
            lambda p, q: dot_tn(left, right[name][:, p * wide : q * wide]), orders[name], 1, wide
        )

    half = hidden_units // 2
    ffn_in = {name: blocks_of(normed_ffn, name) for name in ("x", "y", "z")}
    top_in = {name: blocks_of(out_grad, name) for name in ("x", "y")}
    down_grad = jnp.concatenate(
        [
            column_sum(hidden[:, :half], top_in, "x"),
            column_sum(hidden[:, half:], top_in, "y"),
        ],
        0,
    )
    gate_proj_grad = jnp.concatenate(
        [
            row_sum(ffn_in, gate_grad[:, :half], "z"),
            row_sum(ffn_in, gate_grad[:, half:], "x"),
        ],
        1,
    )
    up_proj_grad = jnp.concatenate(
        [
            row_sum(ffn_in, up_grad[:, :half], "y"),
            row_sum(ffn_in, up_grad[:, half:], "z"),
        ],
        1,
    )

    low_in = {"x": blocks_of(mix_low, "x")}
    output_proj_grad = column_sum(mixed, low_in, "x")
    mixed_grad = jnp.dot(mix_low, output_proj.T, preferred_element_type=F32)
    branch_grad, local_adj, suffix = per_block(
        reverse_kernel,
        rows,
        blocks,
        block,
        ["full"] * 4,
        ["low", "full", "full"],
        [],
        [HALO, 0, 0, 0],
        60,
        (mixed_grad, branch_pre, states, mult),
    )
    first_mult = mult[:1]
    adj_in = carried_in(first_mult * suffix[:1], first_mult * local_adj[:1], -1, rows)
    spread = jnp.zeros((HALO, 1), F32)
    signal_grad, back_edge, dgates_grad, igates_grad, sums = per_block(
        backward_kernel,
        rows,
        blocks,
        block,
        ["full", "full", "edge", "full", "edge", "full", "full", "full", "full", "edge", "mask", "edge", "gate", "gate"],
        ["full", "edge", "gate", "gate", "edge"],
        [HALO, HALO, 2 * HALO],
        [],
        8 * block + 120,
        (
            local_adj,
            suffix,
            adj_in + spread,
            states,
            carry_in + spread,
            conv,
            rgate,
            igate,
            signal,
            edge,
            masks,
            params,
            decay_gates,
            input_gates,
        ),
    )
    edge_back = seq_shift(back_edge, -1)
    signal_low = jnp.concatenate(
        [signal_grad[: rows - HALO], signal_grad[rows - HALO :] + edge_back]
    ).astype(BF16)
    mix_in = {name: blocks_of(normed, name) for name in ("x", "y")}
    branch_proj_grad = row_sum(mix_in, branch_grad, "y")
    input_proj_grad = row_sum(mix_in, signal_low, "x")
    mix_part = jnp.dot(branch_grad, branch_proj.T, preferred_element_type=F32) + jnp.dot(
        signal_low, input_proj.T, preferred_element_type=F32
    )
    mix_norm_grad = mp_sum(mix_part)
    mixer_gain_grad = jnp.sum(mix_norm_grad * mix_unit, axis=0)
    stream_grad = middle_grad + norm_back(mix_norm_grad * mixer_gain, residual, mix_scale)

    own = block // peers

    def per_peer(values):
        return jnp.moveaxis(values.reshape(-1, peers, own), 1, 0).reshape(peers, -1)

    def gate_peer(values):
        return jnp.moveaxis(values.reshape(blocks, peers, own * block), 1, 0).reshape(peers, -1)

    small = [
        gate_peer(dgates_grad),
        gate_peer(igates_grad),
        per_peer(sums),
        mixer_gain_grad.reshape(peers, wide),
        ffn_gain_grad.reshape(peers, wide),
    ]
    sizes = [v.shape[1] for v in small]
    packed = jnp.concatenate(small, 1)
    packed = jnp.pad(packed, ((0, 0), (0, -packed.shape[1] % 1024)))
    summed = lax.psum_scatter(
        packed.reshape(peers, -1, 128), "seq", scatter_dimension=0, tiled=True
    ).reshape(-1)
    pieces = []
    for size in sizes:
        pieces.append(summed[:size])
        summed = summed[size:]
    vectors = pieces[2].reshape(taps + 4, blocks, own)
    gate_shape = (blocks, own, block)
    return (
        result,
        stream_grad,
        pieces[3],
        branch_proj_grad,
        input_proj_grad,
        vectors[:taps],
        vectors[taps],
        pieces[0].reshape(gate_shape),
        vectors[taps + 1],
        pieces[1].reshape(gate_shape),
        vectors[taps + 2],
        vectors[taps + 3],
        output_proj_grad,
        pieces[4],
        gate_proj_grad,
        up_proj_grad,
        down_grad,
    )


def solution(mesh):
    placed = (
        P("seq", None),
        P("seq"),
        P("seq"),
        P(),
        P(None, "mp"),
        P(None, "mp"),
        P(None, "mp", None),
        P("mp", None),
        P("mp", None, None),
        P("mp", None),
        P("mp", None, None),
        P("mp", None),
        P("mp", None),
        P("mp", None),
        P(),
        P(None, "mp"),
        P(None, "mp"),
        P("mp", None),
        P("seq", None),
    )
    return jax.shard_map(
        on_device,
        mesh=mesh,
        in_specs=placed,
        out_specs=(
            P("seq", None),
            P("seq", None),
            P("seq"),
            P("seq", "mp"),
            P("seq", "mp"),
            P(None, "mp", "seq"),
            P("mp", "seq"),
            P("mp", "seq", None),
            P("mp", "seq"),
            P("mp", "seq", None),
            P("mp", "seq"),
            P("mp", "seq"),
            P("mp", "seq"),
            P("seq"),
            P("seq", "mp"),
            P("seq", "mp"),
            P("mp", "seq"),
        ),
        check_vma=False,
    )
```
